256 devices in a mesh: dp: 32 (over y_hi, z, core), head: 8 (over x, y_lo).
Axes of the slice: x: 4, y: 4 (y_hi: 2, y_lo: 2; y = y_hi * 2 + y_lo), z: 8, core: 2. Of those that a mesh axis runs over, the one named last changes fastest.
Arguments:
- queries: bfloat16 [24576, 8192], P(('dp', 'head')), may hold values from -6 to 6, as said below
- key_states: bfloat16 [24576, 1024], P(('dp', 'head')), may hold values from -6 to 6, as said below
- value_states: bfloat16 [24576, 1024], P(('dp', 'head')), may hold values from -6 to 6
- document_lengths: int32 [8], replicated, may hold values from 1 to 12288, 24576 in all
Outputs:
- attended: bfloat16 [24576, 8192], P(('dp', 'head'))
The draws below stay inside these ranges and needn't reach their ends.
Inputs may be any that keep to these rules, and one draw needn't show every extreme that they name: `queries`: within this range. `key_states`: this range. `document_lengths`: the lengths sum to 24576 and the largest is exactly 12288.
All inputs are finite; a program needn't handle non-finite values.
Results may differ from the reference program's by a relative error of at most 0.008.
Values may be sent and summed in bfloat16 or wider, within the bound.
A program may use at most 128 MiB of HBM per device.

```python
import math
import jax
import jax.numpy as jnp
import numpy as np
from jax import lax

HQ = 64
HK = 8
DH = 128
TOK_DEV = 96
DOCS = 8
TOKENS = 24576
DOC_MAX = 12288
N_HEAD = 8


def draw_queries(key, part):
    noise_key = jax.random.fold_in(key, 21)
    base = jnp.clip(jax.random.normal(noise_key, (TOKENS, HQ * DH), jnp.float32), -6.0, 6.0)
    return base.astype(jnp.bfloat16)


def draw_key_states(key, part):
    noise_key = jax.random.fold_in(key, 31)
    base = jnp.clip(jax.random.normal(noise_key, (TOKENS, HK * DH), jnp.float32), -6.0, 6.0)
    return base.astype(jnp.bfloat16)


def shard_levels(rng, extent, cuts, low, top_value):
    level = 1.0
    for dim, blocks in cuts:
        draws = jax.random.uniform(jax.random.fold_in(jax.random.fold_in(rng, 6), dim), (blocks,), jnp.float32, low / len(cuts), top_value / len(cuts))
        level = level * jnp.repeat(jnp.exp(draws), extent[dim] // blocks).reshape((-1,) + (1,) * (len(extent) - 1 - dim))
    return level


def profile(amount, total, limit, skew):
    portions = [(1 << 20) // math.isqrt(standing ** skew) + 1 for standing in range(2, amount + 1)]
    surplus, holding = total - limit - (amount - 1), [1] * (amount - 1)
    while surplus > 0:
        candidates = [i for i in range(amount - 1) if holding[i] < limit]
        pool, budget = sum([portions[i] for i in candidates]), surplus
        for i in candidates:
            addition = min(limit - holding[i], max(1, budget * portions[i] // pool), surplus)
            holding[i] = holding[i] + addition
            surplus = surplus - addition
    return np.array([limit] + holding)


def uneven_parts(key, number_of, total, reach, lean):
    if number_of == 2:
        one = jax.random.randint(key, (), max(1, total - reach), min(reach, total - 1) + 1)
        return jnp.stack([one, total - one])
    tallies = jnp.asarray(profile(number_of, total, reach, lean), jnp.int32)
    pairs = (number_of - 1) // 2
    donor, receiver = tallies[1:1 + 2 * pairs:2], tallies[2:2 + 2 * pairs:2]
    room = jnp.minimum(donor - 1, reach - receiver)
    moved = jax.random.randint(jax.random.fold_in(key, 1), (pairs,), 0, 1 << 20) % (room + 1)
    tallies = tallies.at[1:1 + 2 * pairs:2].set(donor - moved).at[2:2 + 2 * pairs:2].set(receiver + moved)
    return tallies[jax.random.permutation(jax.random.fold_in(key, 2), number_of)]


def scatter_about(rng, shape, width, bound, cuts=(), held_as=jnp.bfloat16):
    gain = shard_levels(rng, shape, cuts, -0.22, 0.18) if cuts else 1.0
    entries = jax.random.normal(rng, shape, jnp.float32) * width * gain
    return jnp.minimum(jnp.maximum(entries, -bound), bound).astype(held_as)


def setup_inputs(seed: int = 0) -> dict:
    key_list = jax.random.split(jax.random.key(seed), 5)
    queries = draw_queries(jax.random.fold_in(key_list[4], 71), 0)
    key_states = draw_key_states(jax.random.fold_in(key_list[4], 71), 0)
    value_states = scatter_about(key_list[2], (TOKENS, HK * DH), 1.0, 6.0, ((0, 256),))
    document_lengths = uneven_parts(key_list[3], DOCS, TOKENS, DOC_MAX, 2).astype(jnp.int32)
    return {"queries": queries, "key_states": key_states, "value_states": value_states, "document_lengths": document_lengths}


def reference(queries, key_states, value_states, document_lengths):
    total_tokens = queries.shape[0]
    block_rows = TOK_DEV * N_HEAD
    window_rows = DOC_MAX + block_rows
    group_heads = HQ // HK
    document_ends = jnp.cumsum(document_lengths).astype(jnp.int32)
    positions = jnp.arange(total_tokens, dtype=jnp.int32)
    document_start = jnp.sum(jnp.where(document_ends[None, :] <= positions[:, None], document_lengths[None, :], 0), axis=1).astype(jnp.int32)
    query_heads = queries.reshape(total_tokens, HK, group_heads, DH)
    key_heads = key_states.reshape(total_tokens, HK, DH)
    value_heads = value_states.reshape(total_tokens, HK, DH)
    score_scale = DH ** -0.5

    def one_block(block_number):
        first_row = (block_number * block_rows).astype(jnp.int32)
        lowest = jnp.maximum(first_row + block_rows - window_rows, 0).astype(jnp.int32)
        query_block = lax.dynamic_slice_in_dim(query_heads, first_row, block_rows, 0)
        key_block = lax.dynamic_slice_in_dim(key_heads, lowest, window_rows, 0)
        value_block = lax.dynamic_slice_in_dim(value_heads, lowest, window_rows, 0)
        query_positions = first_row + jnp.arange(block_rows, dtype=jnp.int32)
        key_positions = lowest + jnp.arange(window_rows, dtype=jnp.int32)
        query_starts = lax.dynamic_slice_in_dim(document_start, first_row, block_rows, 0)
        allowed = (key_positions[None, :] <= query_positions[:, None]) & (key_positions[None, :] >= query_starts[:, None])

        def one_head(head_number):
            query_rows = jnp.take(query_block, head_number, axis=1).astype(jnp.float32)
            key_rows = jnp.take(key_block, head_number, axis=1).astype(jnp.float32)
            value_rows = jnp.take(value_block, head_number, axis=1).astype(jnp.float32)
            scores = jnp.einsum("qgd,kd->qgk", query_rows, key_rows) * score_scale
            scores = jnp.where(allowed[:, None, :], scores, -jnp.inf)
            highest = jnp.max(scores, axis=2, keepdims=True)
            weights = jnp.exp(scores - highest)
            totals = jnp.sum(weights, axis=2)
            weights_low = lax.optimization_barrier(weights.astype(jnp.bfloat16)).astype(jnp.float32)
            summed = jnp.einsum("qgk,kd->qgd", weights_low, value_rows)
            return summed / totals[:, :, None]

        results = lax.map(one_head, jnp.arange(HK, dtype=jnp.int32))
        return jnp.transpose(results, (1, 0, 2, 3)).reshape(block_rows, HQ * DH).astype(jnp.bfloat16)

    blocks = lax.map(one_block, jnp.arange(total_tokens // block_rows, dtype=jnp.int32))
    return blocks.reshape(total_tokens, HQ * DH)
```

```python
import functools

import jax
import jax.numpy as jnp
from jax import lax
from jax.experimental import pallas as pl
from jax.experimental.pallas import tpu as pltpu
from jax.sharding import PartitionSpec as P

HQ = 64
HK = 8
DH = 128
DOCS = 8
TOK = 96
BLOCK = 8 * TOK
TOKENS = 32 * BLOCK
PLANES = 8
GROUP = HQ // HK
HALF = GROUP // 2
WIDE = HALF * DH
TQ = 256
KT = 1024
KS = 256
SCALE = DH**-0.5 * 1.4426950408889634
BOUND = 60.0
MESH = pl.DeviceIdType.MESH
VMEM_LIMIT = 60 * 1024 * 1024


def place():
    dp = lax.axis_index("dp")
    return dp, dp // 16, (dp % 16) // 2, dp % 2, lax.axis_index("head")


def dp_of(y_hi, z, core):
    return y_hi * 16 + z * 2 + core


def rows_of(dp, first=0, count=BLOCK):
    return pl.ds(pl.multiple_of(dp * BLOCK + first, 32), count)


def gather_kernel(
    q_ref, k_ref, v_ref, q_out, k_out, v_out, a_send, a_recv, r_send, r_recv, c_send, c_recv, l_sem
):
    dp, y_hi, z, core, head = place()

    def remote(src, dst, send, recv, to_dp, to_head):
        return pltpu.make_async_remote_copy(
            src_ref=src, dst_ref=dst, send_sem=send, recv_sem=recv,
            device_id=(to_dp, to_head), device_id_type=MESH,
        )

    peers = []
    for j in range(16):
        peers.append((dp_of((y_hi + j // 8) % 2, z, core), (head + j % 8) % 8, (y_hi + j // 8) % 2))
    up = dp_of(y_hi, (z + 1) % PLANES, core)
    down = dp_of(y_hi, (z + PLANES - 1) % PLANES, core)
    twin = dp_of(y_hi, z, 1 - core)

    barrier = pltpu.get_barrier_semaphore()
    for to_dp, to_head, _ in peers[1:]:
        pl.semaphore_signal(barrier, inc=1, device_id=(to_dp, to_head), device_id_type=MESH)
    for to_dp in (up, down, twin):
        pl.semaphore_signal(barrier, inc=1, device_id=(to_dp, head), device_id_type=MESH)
    pl.semaphore_wait(barrier, 18)

    sent = []
    outs = (k_out, v_out)
    own_rows = rows_of(dp, head * TOK, TOK)

    def columns(first, width):
        return pl.ds(pl.multiple_of(first, 128), width)

    local = []
    for i, ref in enumerate((k_ref, v_ref)):
        local.append(pltpu.make_async_copy(
            ref.at[:, columns(head * DH, DH)], outs[i].at[own_rows, :], l_sem.at[i]))
    local.append(pltpu.make_async_copy(
        q_ref.at[:, columns((head * 2 + y_hi) * WIDE, WIDE)],
        q_out.at[pl.ds(pl.multiple_of(y_hi * BLOCK + head * TOK, 32), TOK), :], l_sem.at[2]))
    for copy in local:
        copy.start()
    entry = {}
    for j in range(1, 16):
        to_dp, to_head, _ = peers[j]
        for i, ref in enumerate((k_ref, v_ref)):
            entry[i, j] = remote(ref.at[:, columns(to_head * DH, DH)], outs[i].at[own_rows, :],
                                 a_send.at[i, j], a_recv.at[i, j], to_dp, to_head)
            entry[i, j].start()
    for j in range(1, 16):
        to_dp, to_head, to_y = peers[j]
        entry[2, j] = remote(
            q_ref.at[:, columns((to_head * 2 + to_y) * WIDE, WIDE)],
            q_out.at[pl.ds(pl.multiple_of(y_hi * BLOCK + head * TOK, 32), TOK), :],
            a_send.at[2, j], a_recv.at[2, j], to_dp, to_head)
        entry[2, j].start()

    def piece(plane, t, i):
        return outs[i].at[rows_of(dp_of((y_hi + t) % 2, plane, core)), :]

    ring, cross = {}, {}

    def pass_on(s, t, i, way):
        plane = (z + PLANES - s) % PLANES if way == 0 else (z + s) % PLANES
        part = piece(plane, t, i)
        if s < 3 or (s == 3 and way == i):
            copy = remote(part, part, r_send.at[way, s, 2 * t + i], r_recv.at[way, s, 2 * t + i],
                          up if way == 0 else down, head)
            copy.start()
            ring[way, s, t, i] = copy
        return part

    def to_twin(part, slot, t, i):
        copy = remote(part, part, c_send.at[slot, 2 * t + i], c_recv.at[slot, 2 * t + i], twin, head)
        copy.start()
        cross[slot, t, i] = copy

    for t in range(2):
        for i in range(2):
            if t == 0:
                local[i].wait()
            for j in range(8 * t, 8 * t + 8):
                if j:
                    entry[i, j].wait_recv()
            part = pass_on(0, t, i, 0)
            pass_on(0, t, i, 1)
            to_twin(part, 0, t, i)
    for s in range(1, 5):
        for t in range(2):
            for i in range(2):
                for way in range(2):
                    if s == 4 and way != i:
                        continue
                    ring[way, s - 1, t, i].wait_recv()
                    part = pass_on(s, t, i, way)
                    to_twin(part, s if way == 0 or s == 4 else 4 + s, t, i)
    local[2].wait()
    for key, copy in entry.items():
        if key[0] == 2:
            copy.wait_recv()
    for copy in cross.values():
        copy.wait_recv()
    for group in (entry, ring, cross):
        for copy in group.values():
            copy.wait_send()


def gather(q, k, v):
    return pl.pallas_call(
        gather_kernel,
        out_shape=(
            jax.ShapeDtypeStruct((2 * BLOCK, WIDE), jnp.bfloat16),
            jax.ShapeDtypeStruct((TOKENS, DH), jnp.bfloat16),
            jax.ShapeDtypeStruct((TOKENS, DH), jnp.bfloat16),
        ),
        in_specs=[pl.BlockSpec(memory_space=pltpu.VMEM)] * 3,
        out_specs=[pl.BlockSpec(memory_space=pl.ANY)] * 3,
        scratch_shapes=[
            pltpu.SemaphoreType.DMA((3, 16)),
            pltpu.SemaphoreType.DMA((3, 16)),
            pltpu.SemaphoreType.DMA((2, 4, 4)),
            pltpu.SemaphoreType.DMA((2, 4, 4)),
            pltpu.SemaphoreType.DMA((8, 4)),
            pltpu.SemaphoreType.DMA((8, 4)),
            pltpu.SemaphoreType.DMA((3,)),
        ],
        compiler_params=pltpu.CompilerParams(collective_id=0, has_side_effects=True),
        name="gather",
    )(q, k, v)


def largest_square(ref, rows, columns):
    ones = jnp.ones((DH, DH), jnp.bfloat16)

    def step(n, top):
        part = ref[pl.ds(pl.multiple_of(n * 512, 512), 512), columns].astype(jnp.float32)
        squares = jnp.dot((part * part).astype(jnp.bfloat16), ones, preferred_element_type=jnp.float32)
        return jnp.maximum(top, jnp.max(squares.reshape(64, 8, DH), axis=0))

    top = lax.fori_loop(0, rows // 512, step, jnp.zeros((8, DH), jnp.float32))
    return jnp.max(top) * 1.02


def attend_kernel(lengths, q_ref, k_ref, v_ref, o_ref, acc, tot, top):
    _, _, z, core, _ = place()
    ends = []
    running = jnp.int32(0)
    for d in range(DOCS):
        running = running + lengths[d]
        ends.append(running)

    def start_of(position):
        return sum(jnp.where(ends[d] <= position, lengths[d], 0) for d in range(DOCS))

    q_top = functools.reduce(
        jnp.maximum, [largest_square(q_ref, 2 * BLOCK, slice(g * DH, (g + 1) * DH)) for g in range(HALF)]
    )
    k_top = largest_square(k_ref, TOKENS, slice(0, DH))
    small = q_top * k_top <= (BOUND * DH**0.5) ** 2

    def fold(row, first, width, masked, shifted):
        key_rows = pl.ds(pl.multiple_of(first, KS), width)
        keys, values = k_ref[key_rows, :], v_ref[key_rows, :]
        if masked:
            positions = row[1] + lax.broadcasted_iota(jnp.int32, (TQ, 1), 0)
            starts = start_of(positions)
            key_positions = first + lax.broadcasted_iota(jnp.int32, (1, width), 1)
            allowed = (key_positions <= positions) & (key_positions >= starts)
        for g in range(HALF):
            part = pl.ds(g * TQ, TQ)
            scores = lax.dot_general(
                q_ref[pl.ds(pl.multiple_of(row[0], TQ), TQ), g * DH : (g + 1) * DH], keys,
                (((1,), (1,)), ((), ())), preferred_element_type=jnp.float32) * SCALE
            if shifted:
                if masked:
                    scores = jnp.where(allowed, scores, -1e30)
                old = top[part, :]
                new = jnp.maximum(old, jnp.max(scores, axis=1, keepdims=True))
                top[part, :] = new
                weights = jnp.exp2(scores - new[:, :1])
                factor = jnp.exp2(old - new)
            else:
                weights = jnp.exp2(scores)
            if masked:
                weights = jnp.where(allowed, weights, 0.0)
            sums = weights[:, :DH]
            for n in range(1, width // DH):
                sums = sums + weights[:, n * DH : (n + 1) * DH]
            product = jnp.dot(weights.astype(jnp.bfloat16), values, preferred_element_type=jnp.float32)
            if shifted:
                tot[part, :] = tot[part, :] * factor + sums
                acc[part, :] = acc[part, :] * factor + product
            else:
                tot[part, :] += sums
                acc[part, :] += product

    def run(shifted):
        def tile(n, carry):
            block, inner = n // (BLOCK // TQ), n % (BLOCK // TQ)
            row = (n * TQ, dp_of(block, z, core) * BLOCK + inner * TQ)
            acc[...] = jnp.zeros_like(acc)
            tot[...] = jnp.zeros_like(tot)
            if shifted:
                top[...] = jnp.full_like(top, -1e30)
            begin = row[1] // KS
            low = start_of(row[1]) // KS
            high = jnp.minimum((start_of(row[1] + TQ - 1) + KS - 1) // KS, begin)
            wide = (begin - high) // (KT // KS)

            def at(width, masked, base):
                def body(i, c):
                    fold(row, (base + i * (width // KS)) * KS, width, masked, shifted)
                    return c
                return body

            lax.fori_loop(0, high - low, at(KS, True, low), 0)
            lax.fori_loop(0, wide, at(KT, False, high), 0)
            rest = high + wide * (KT // KS)
            lax.fori_loop(0, begin - rest, at(KS, False, rest), 0)
            fold(row, row[1], TQ, True, shifted)
            for g in range(HALF):
                part = pl.ds(g * TQ, TQ)
                total = jnp.sum(tot[part, :], axis=1, keepdims=True)
                o_ref[pl.ds(pl.multiple_of(row[0], TQ), TQ), g * DH : (g + 1) * DH] = (
                    acc[part, :] / total).astype(jnp.bfloat16)
            return carry

        lax.fori_loop(0, 2 * BLOCK // TQ, tile, 0)

    @pl.when(small)
    def _():
        run(False)

    @pl.when(jnp.logical_not(small))
    def _():
        run(True)


def attend(lengths, q, k, v):
    return pl.pallas_call(
        attend_kernel,
        out_shape=jax.ShapeDtypeStruct((2 * BLOCK, WIDE), jnp.bfloat16),
        in_specs=[pl.BlockSpec(memory_space=pltpu.SMEM)] + [pl.BlockSpec(memory_space=pltpu.VMEM)] * 3,
        out_specs=pl.BlockSpec(memory_space=pltpu.VMEM),
        scratch_shapes=[pltpu.VMEM((HALF * TQ, DH), jnp.float32)] * 3,
        compiler_params=pltpu.CompilerParams(vmem_limit_bytes=VMEM_LIMIT),
        name="attend",
    )(lengths, q, k, v)


def scatter_kernel(o_ref, out_ref, send, recv, l_sem):
    dp, y_hi, z, core, head = place()
    peers = []
    for j in range(16):
        to_y = (y_hi + j // 8) % 2
        peers.append((dp_of(to_y, z, core), (head + j % 8) % 8, to_y))
    barrier = pltpu.get_barrier_semaphore()
    for to_dp, to_head, _ in peers[1:]:
        pl.semaphore_signal(barrier, inc=1, device_id=(to_dp, to_head), device_id_type=MESH)
    pl.semaphore_wait(barrier, 15)
    columns = pl.ds(pl.multiple_of((head * 2 + y_hi) * WIDE, 128), WIDE)
    copies = []
    for j in range(16):
        to_dp, to_head, to_y = peers[j]
        src = o_ref.at[pl.ds(pl.multiple_of(to_y * BLOCK + to_head * TOK, 32), TOK), :]
        if j == 0:
            copies.append(pltpu.make_async_copy(src, out_ref.at[:, columns], l_sem))
        else:
            copies.append(pltpu.make_async_remote_copy(
                src_ref=src, dst_ref=out_ref.at[:, columns], send_sem=send.at[j], recv_sem=recv.at[j],
                device_id=(to_dp, to_head), device_id_type=MESH))
        copies[-1].start()
    for copy in copies:
        copy.wait()


def scatter(o):
    return pl.pallas_call(
        scatter_kernel,
        out_shape=jax.ShapeDtypeStruct((TOK, HQ * DH), jnp.bfloat16),
        in_specs=[pl.BlockSpec(memory_space=pl.ANY)],
        out_specs=pl.BlockSpec(memory_space=pl.ANY),
        scratch_shapes=[
            pltpu.SemaphoreType.DMA((16,)),
            pltpu.SemaphoreType.DMA((16,)),
            pltpu.SemaphoreType.DMA(()),
        ],
        compiler_params=pltpu.CompilerParams(collective_id=1, has_side_effects=True),
        name="scatter",
    )(o)


def on_device(queries, key_states, value_states, document_lengths):
    q, k, v = gather(queries, key_states, value_states)
    return scatter(attend(document_lengths, q, k, v))


def solution(mesh):
    placed = (P(("dp", "head"), None), P(("dp", "head"), None), P(("dp", "head"), None), P())
    return jax.shard_map(
        on_device, mesh=mesh, in_specs=placed, out_specs=P(("dp", "head"), None), check_vma=False
    )
```

```python
import jax
import jax.numpy as jnp
from jax import lax
from jax.experimental import pallas as pl
from jax.experimental.pallas import tpu as pltpu
from jax.sharding import PartitionSpec as P

HQ = 64
HK = 8
DH = 128
DOCS = 8
TOK = 96
BLOCK = 8 * TOK
TOKENS = 32 * BLOCK
PLANES = 8
GROUP = HQ // HK
HALF = GROUP // 2
WIDE = HALF * DH
TQ = 256
KT = 1024
KS = 256
SCALE = DH**-0.5 * 1.4426950408889634
BOUND = 60.0
MESH = pl.DeviceIdType.MESH
VMEM_LIMIT = 32 * 1024 * 1024


def place():
    dp = lax.axis_index("dp")
    return dp, dp // 16, (dp % 16) // 2, dp % 2, lax.axis_index("head")


def dp_of(y_hi, z, core):
    return y_hi * 16 + z * 2 + core


def squares_top(ref, first, rows, columns):
    ones = jnp.ones((DH, DH), jnp.bfloat16)

    def step(n, top):
        part = ref[pl.ds(pl.multiple_of(first + n * 384, 32), 384), columns].astype(jnp.float32)
        squares = jnp.dot((part * part).astype(jnp.bfloat16), ones, preferred_element_type=jnp.float32)
        return jnp.maximum(top, jnp.max(squares.reshape(48, 8, DH), axis=0))

    return lax.fori_loop(0, rows // 384, step, jnp.zeros((8, DH), jnp.float32))


def gather_kernel(
    q_ref, k_ref, v_ref, q_out, kv_out, top_out,
    a_send, a_recv, r_send, r_recv, y_send, y_recv, c_send, c_recv, l_sem
):
    dp, y_hi, z, core, head = place()
    x, y_lo = head // 2, head % 2

    def remote(src, dst, send, recv, to_dp, to_head):
        return pltpu.make_async_remote_copy(
            src_ref=src, dst_ref=dst, send_sem=send, recv_sem=recv,
            device_id=(to_dp, to_head), device_id_type=MESH,
        )

    def shifted(j):
        return (y_hi + j // 8) % 2, (head + j % 8) % 8

    up = dp_of(y_hi, (z + 1) % PLANES, core)
    down = dp_of(y_hi, (z + PLANES - 1) % PLANES, core)
    twin = dp_of(y_hi, z, 1 - core)
    side = x * 2 + 1 - y_lo

    barrier = pltpu.get_barrier_semaphore()
    for j in range(1, 16):
        to_y, to_head = shifted(j)
        pl.semaphore_signal(
            barrier, inc=1, device_id=(dp_of(to_y, z, core), to_head), device_id_type=MESH)
    for to_dp in (up, down, twin):
        pl.semaphore_signal(barrier, inc=1, device_id=(to_dp, head), device_id_type=MESH)
    pl.semaphore_wait(barrier, 18)

    def columns(first, width):
        return pl.ds(pl.multiple_of(first, 128), width)

    def entry_ends(i, to_y, to_head):
        kv_head = to_head // 2 * 2 + to_y
        if i == 2:
            src = q_ref.at[:, columns((kv_head * 2 + to_head % 2) * WIDE, WIDE)]
            return src, q_out.at[pl.ds(pl.multiple_of(y_hi * BLOCK + head * TOK, 32), TOK), :]
        src = (k_ref, v_ref)[i].at[:, columns(kv_head * DH, DH)]
        return src, kv_out.at[pl.ds(pl.multiple_of(i * TOKENS + dp * BLOCK + head * TOK, 32), TOK), :]

    local, entry = [], {}
    for i in range(3):
        src, dst = entry_ends(i, y_hi, head)
        local.append(pltpu.make_async_copy(src, dst, l_sem.at[i]))
        local[-1].start()
    for kinds in ((0, 1), (2,)):
        for j in range(1, 16):
            to_y, to_head = shifted(j)
            for i in kinds:
                src, dst = entry_ends(i, to_y, to_head)
                entry[i, j] = remote(
                    src, dst, a_send.at[i, j], a_recv.at[i, j], dp_of(to_y, z, core), to_head)
                entry[i, j].start()

    def part_at(plane, e, of_core):
        first = (e % 2) * TOKENS + dp_of((y_hi + e // 2) % 2, plane, of_core) * BLOCK
        return kv_out.at[pl.ds(pl.multiple_of(first, 32), BLOCK), :]

    def plane_of(slot):
        return (z + PLANES - slot) % PLANES if slot <= 4 else (z + slot - 4) % PLANES

    ring, aside, cross = {}, {}, {}
    missing, shared = 3 * (1 - y_lo), 3 * y_lo

    def to_twin(slot, n, e):
        part = part_at(plane_of(slot), e, core)
        cross[slot, n] = remote(part, part, c_send.at[slot, n], c_recv.at[slot, n], twin, head)
        cross[slot, n].start()

    def along(way, s, r):
        slot = s if way == 0 or s == 0 else 4 + s
        part = part_at(plane_of(slot), y_lo + r, core)
        ring[way, s, r] = remote(
            part, part, r_send.at[way, s, r], r_recv.at[way, s, r], up if way == 0 else down, head)
        ring[way, s, r].start()

    def to_side(slot):
        part = part_at(plane_of(slot), shared, core)
        aside[slot] = remote(part, part, y_send.at[slot], y_recv.at[slot], dp, side)
        aside[slot].start()

    def last_way(r):
        return 0 if r < 2 else 1

    top_out[...] = jnp.zeros_like(top_out)

    def look(slot, of_core):
        for t in range(2):
            first = dp_of((y_hi + t) % 2, plane_of(slot), of_core) * BLOCK
            top_out[0, :, :] = jnp.maximum(top_out[0, :, :], squares_top(kv_out, first, BLOCK, slice(0, DH)))

    for i in range(2):
        local[i].wait()
        for j in range(1, 16):
            entry[i, j].wait_recv()
    for r in range(3):
        along(0, 0, r)
        along(1, 0, r)
    for n in range(4):
        to_twin(0, n, n)
    look(0, core)

    def slots_of(s):
        return (s,) if s in (0, 4) else (s, 4 + s)

    def settle(s):
        for slot in slots_of(s):
            if s:
                aside[slot].wait_recv()
                to_twin(slot, 3, missing)
                look(slot, core)

    def close(s):
        for slot in slots_of(s):
            for n in range(4):
                cross[slot, n].wait_recv()
            look(slot, 1 - core)

    for s in range(1, 5):
        for r in range(3):
            for way in range(2):
                if s == 4 and way != last_way(r):
                    continue
                slot = s if way == 0 or s == 4 else 4 + s
                ring[way, s - 1, r].wait_recv()
                if s < 3 or (s == 3 and way == last_way(r)):
                    along(way, s, r)
                to_twin(slot, r, y_lo + r)
        for slot in slots_of(s):
            to_side(slot)
        if s == 2:
            local[2].wait()
            for j in range(1, 16):
                entry[2, j].wait_recv()
            for g in range(HALF):
                top_out[1, :, :] = jnp.maximum(
                    top_out[1, :, :], squares_top(q_out, 0, 2 * BLOCK, slice(g * DH, (g + 1) * DH)))
        settle(s - 1)
        close(s - 1)
    settle(4)
    close(4)
    for group in (entry, ring, aside, cross):
        for copy in group.values():
            copy.wait_send()


def gather(q, k, v):
    return pl.pallas_call(
        gather_kernel,
        out_shape=(
            pltpu.VMEM((2 * BLOCK, WIDE), jnp.bfloat16),
            pltpu.VMEM((2 * TOKENS, DH), jnp.bfloat16),
            pltpu.VMEM((2, 8, DH), jnp.float32),
        ),
        in_specs=[pl.BlockSpec(memory_space=pltpu.VMEM)] * 3,
        out_specs=[pl.BlockSpec(memory_space=pltpu.VMEM)] * 3,
        scratch_shapes=[
            pltpu.SemaphoreType.DMA((3, 16)),
            pltpu.SemaphoreType.DMA((3, 16)),
            pltpu.SemaphoreType.DMA((2, 4, 3)),
            pltpu.SemaphoreType.DMA((2, 4, 3)),
            pltpu.SemaphoreType.DMA((8,)),
            pltpu.SemaphoreType.DMA((8,)),
            pltpu.SemaphoreType.DMA((8, 4)),
            pltpu.SemaphoreType.DMA((8, 4)),
            pltpu.SemaphoreType.DMA((3,)),
        ],
        compiler_params=pltpu.CompilerParams(
            collective_id=0, has_side_effects=True, vmem_limit_bytes=24 * 1024 * 1024),
        name="gather",
    )(q, k, v)


def attend_kernel(lengths, q_ref, kv_ref, tops_ref, o_ref, acc, tot, top):
    _, _, z, core, _ = place()
    ends = []
    running = jnp.int32(0)
    for d in range(DOCS):
        running = running + lengths[d]
        ends.append(running)

    def start_of(position):
        return sum(jnp.where(ends[d] <= position, lengths[d], 0) for d in range(DOCS))

    q_top, k_top = jnp.max(tops_ref[1, :, :]), jnp.max(tops_ref[0, :, :])
    small = q_top * k_top * 1.04 <= (BOUND * DH**0.5) ** 2

    def fold(row, first, width, masked, shifted):
        keys = kv_ref[pl.ds(pl.multiple_of(first, KS), width), :]
        values = kv_ref[pl.ds(pl.multiple_of(TOKENS + first, KS), width), :]
        if masked:
            positions = row[1] + lax.broadcasted_iota(jnp.int32, (TQ, 1), 0)
            starts = start_of(positions)
            key_positions = first + lax.broadcasted_iota(jnp.int32, (1, width), 1)
            allowed = (key_positions <= positions) & (key_positions >= starts)
        for g in range(HALF):
            part = pl.ds(g * TQ, TQ)
            scores = lax.dot_general(
                q_ref[pl.ds(pl.multiple_of(row[0], TQ), TQ), g * DH : (g + 1) * DH], keys,
                (((1,), (1,)), ((), ())), preferred_element_type=jnp.float32) * SCALE
            if shifted:
                if masked:
                    scores = jnp.where(allowed, scores, -1e30)
                old = top[part, :]
                new = jnp.maximum(old, jnp.max(scores, axis=1, keepdims=True))
                top[part, :] = new
                weights = jnp.exp2(scores - new[:, :1])
                factor = jnp.exp2(old - new)
            else:
                weights = jnp.exp2(scores)
            if masked:
                weights = jnp.where(allowed, weights, 0.0)
            sums = weights[:, :DH]
            for n in range(1, width // DH):
                sums = sums + weights[:, n * DH : (n + 1) * DH]
            product = jnp.dot(weights.astype(jnp.bfloat16), values, preferred_element_type=jnp.float32)
            if shifted:
                tot[part, :] = tot[part, :] * factor + sums
                acc[part, :] = acc[part, :] * factor + product
            else:
                tot[part, :] += sums
                acc[part, :] += product

    def run(shifted):
        def tile(n, carry):
            block, inner = n // (BLOCK // TQ), n % (BLOCK // TQ)
            row = (n * TQ, dp_of(block, z, core) * BLOCK + inner * TQ)
            acc[...] = jnp.zeros_like(acc)
            tot[...] = jnp.zeros_like(tot)
            if shifted:
                top[...] = jnp.full_like(top, -1e30)
            begin = row[1] // KS
            low = start_of(row[1]) // KS
            high = jnp.minimum((start_of(row[1] + TQ - 1) + KS - 1) // KS, begin)
            wide = (begin - high) // (KT // KS)

            def at(width, masked, base):
                def body(i, c):
                    fold(row, (base + i * (width // KS)) * KS, width, masked, shifted)
                    return c
                return body

            lax.fori_loop(0, high - low, at(KS, True, low), 0)
            lax.fori_loop(0, wide, at(KT, False, high), 0)
            rest = high + wide * (KT // KS)
            lax.fori_loop(0, begin - rest, at(KS, False, rest), 0)
            fold(row, row[1], TQ, True, shifted)
            for g in range(HALF):
                part = pl.ds(g * TQ, TQ)
                total = jnp.sum(tot[part, :], axis=1, keepdims=True)
                o_ref[pl.ds(pl.multiple_of(row[0], TQ), TQ), g * DH : (g + 1) * DH] = (
                    acc[part, :] / total).astype(jnp.bfloat16)
            return carry

        lax.fori_loop(0, 2 * BLOCK // TQ, tile, 0)

    @pl.when(small)
    def _():
        run(False)

    @pl.when(jnp.logical_not(small))
    def _():
        run(True)


def attend(lengths, q, kv, tops):
    q, kv, tops = (pltpu.with_memory_space_constraint(a, pltpu.VMEM) for a in (q, kv, tops))
    return pl.pallas_call(
        attend_kernel,
        out_shape=pltpu.VMEM((2 * BLOCK, WIDE), jnp.bfloat16),
        in_specs=[pl.BlockSpec(memory_space=pltpu.SMEM)] + [pl.BlockSpec(memory_space=pltpu.VMEM)] * 3,
        out_specs=pl.BlockSpec(memory_space=pltpu.VMEM),
        scratch_shapes=[pltpu.VMEM((HALF * TQ, DH), jnp.float32)] * 3,
        compiler_params=pltpu.CompilerParams(vmem_limit_bytes=VMEM_LIMIT),
        name="attend",
    )(lengths, q, kv, tops)


def scatter_kernel(o_ref, out_ref, send, recv, l_sem):
    dp, y_hi, z, core, head = place()
    peers = []
    for j in range(16):
        to_y = (y_hi + j // 8) % 2
        peers.append((dp_of(to_y, z, core), (head + j % 8) % 8, to_y))
    barrier = pltpu.get_barrier_semaphore()
    for to_dp, to_head, _ in peers[1:]:
        pl.semaphore_signal(barrier, inc=1, device_id=(to_dp, to_head), device_id_type=MESH)
    pl.semaphore_wait(barrier, 15)
    kv_head = head // 2 * 2 + y_hi
    columns = pl.ds(pl.multiple_of((kv_head * 2 + head % 2) * WIDE, 128), WIDE)
    copies = []
    for j in range(16):
        to_dp, to_head, to_y = peers[j]
        src = o_ref.at[pl.ds(pl.multiple_of(to_y * BLOCK + to_head * TOK, 32), TOK), :]
        if j == 0:
            copies.append(pltpu.make_async_copy(src, out_ref.at[:, columns], l_sem))
        else:
            copies.append(pltpu.make_async_remote_copy(
                src_ref=src, dst_ref=out_ref.at[:, columns], send_sem=send.at[j], recv_sem=recv.at[j],
                device_id=(to_dp, to_head), device_id_type=MESH))
        copies[-1].start()
    for copy in copies:
        copy.wait()


def scatter(o):
    return pl.pallas_call(
        scatter_kernel,
        out_shape=jax.ShapeDtypeStruct((TOK, HQ * DH), jnp.bfloat16),
        in_specs=[pl.BlockSpec(memory_space=pltpu.VMEM)],
        out_specs=pl.BlockSpec(memory_space=pl.ANY),
        scratch_shapes=[
            pltpu.SemaphoreType.DMA((16,)),
            pltpu.SemaphoreType.DMA((16,)),
            pltpu.SemaphoreType.DMA(()),
        ],
        compiler_params=pltpu.CompilerParams(collective_id=1, has_side_effects=True),
        name="scatter",
    )(pltpu.with_memory_space_constraint(o, pltpu.VMEM))


def on_device(queries, key_states, value_states, document_lengths):
    return scatter(attend(document_lengths, *gather(queries, key_states, value_states)))


def solution(mesh):
    placed = (P(("dp", "head"), None), P(("dp", "head"), None), P(("dp", "head"), None), P())
    return jax.shard_map(
        on_device, mesh=mesh, in_specs=placed, out_specs=P(("dp", "head"), None), check_vma=False
    )
```

```python
import jax
import jax.numpy as jnp
from jax import lax
from jax.experimental import pallas as pl
from jax.experimental.pallas import tpu as pltpu
from jax.sharding import PartitionSpec as P

HQ = 64
HK = 8
DH = 128
DOCS = 8
TOK = 96
BLOCK = 8 * TOK
TOKENS = 32 * BLOCK
PLANES = 8
GROUP = HQ // HK
HALF = GROUP // 2
WIDE = HALF * DH
TQ = 256
KT = 1024
KS = 256
MASKED = -1e30
NEAR = 2
SCALE = DH**-0.5 * 1.4426950408889634
BOUND = 60.0
MESH = pl.DeviceIdType.MESH
VMEM_LIMIT = 16 * 1024 * 1024


def place():
    dp = lax.axis_index("dp")
    return dp, dp // 16, (dp % 16) // 2, dp % 2, lax.axis_index("head")


def dp_of(y_hi, z, core):
    return y_hi * 16 + z * 2 + core


def starts(lengths):
    ends = []
    running = jnp.int32(0)
    for d in range(DOCS):
        running = running + lengths[d]
        ends.append(running)
    return lambda position: sum(jnp.where(ends[d] <= position, lengths[d], 0) for d in range(DOCS))


def second_first(start_of, z, core):
    first, second = (dp_of(t, z, core) * BLOCK + BLOCK - 1 for t in range(2))
    return second - start_of(second) > first - start_of(first)


def squares_top(ref, first, rows, columns):
    ones = jnp.ones((DH, DH), jnp.bfloat16)

    def step(n, top):
        part = ref[pl.ds(pl.multiple_of(first + n * 384, 32), 384), columns].astype(jnp.float32)
        squares = jnp.dot((part * part).astype(jnp.bfloat16), ones, preferred_element_type=jnp.float32)
        return jnp.maximum(top, jnp.max(squares.reshape(48, 8, DH), axis=0))

    return lax.fori_loop(0, rows // 384, step, jnp.zeros((8, DH), jnp.float32))


def gather_kernel(
    lengths, q_ref, k_ref, v_ref, q_out, kv_out, top_out, acc_out, tot_out,
    kv_own, bias, a_send, a_recv, q_send, q_recv, r_send, r_recv, c_send, c_recv, l_sem
):
    dp, y_hi, z, core, head = place()

    def remote(src, dst, send, recv, to_dp, to_head):
        return pltpu.make_async_remote_copy(
            src_ref=src, dst_ref=dst, send_sem=send, recv_sem=recv,
            device_id=(to_dp, to_head), device_id_type=MESH,
        )

    def shifted(j):
        return (y_hi + j // 8) % 2, (head + j % 8) % 8

    up = dp_of(y_hi, (z + 1) % PLANES, core)
    down = dp_of(y_hi, (z + PLANES - 1) % PLANES, core)
    twin = dp_of(y_hi, z, 1 - core)

    def columns(first, width):
        return pl.ds(pl.multiple_of(first, 128), width)

    def q_place(to_y, to_head):
        src = q_ref.at[:, columns(((to_head // 2 * 2 + to_y) * 2 + to_head % 2) * WIDE, WIDE)]
        return src, q_out.at[pl.ds(pl.multiple_of(y_hi * BLOCK + head * TOK, 32), TOK), :]

    loads = [pltpu.make_async_copy(ref, kv_own.at[pl.ds(i * TOK, TOK), :], l_sem.at[i])
             for i, ref in enumerate((k_ref, v_ref))]
    for load in loads:
        load.start()
    barrier = pltpu.get_barrier_semaphore()
    for j in range(1, 16):
        to_y, to_head = shifted(j)
        pl.semaphore_signal(
            barrier, inc=1, device_id=(dp_of(to_y, z, core), to_head), device_id_type=MESH)
    for to_dp in (up, down, twin):
        pl.semaphore_signal(barrier, inc=1, device_id=(to_dp, head), device_id_type=MESH)
    own_q = q_place(y_hi, head)
    own_copy = pltpu.make_async_copy(own_q[0], own_q[1], l_sem.at[2])
    own_copy.start()
    for load in loads:
        load.wait()
    pl.semaphore_wait(barrier, 18)

    def class_ends(e, to_y, to_head):
        i = e % 2
        src = kv_own.at[pl.ds(pl.multiple_of(i * TOK, 32), TOK), columns((to_head // 2 * 2 + to_y) * DH, DH)]
        return src, kv_out.at[pl.ds(pl.multiple_of(i * TOKENS + dp * BLOCK + head * TOK, 32), TOK), :]

    entry = {}
    for e in range(4):
        to_y = (y_hi + e // 2) % 2
        for j in range(8):
            to_head = (head + j) % 8
            src, dst = class_ends(e, to_y, to_head)
            if j or e >= 2:
                entry[e, j] = remote(
                    src, dst, a_send.at[e, j], a_recv.at[e, j], dp_of(to_y, z, core), to_head)
            else:
                entry[e, j] = pltpu.make_async_copy(src, dst, l_sem.at[3 + e])
            entry[e, j].start()
    for j in range(1, 16):
        to_y, to_head = shifted(j)
        src, dst = q_place(to_y, to_head)
        entry[4, j] = remote(src, dst, q_send.at[j], q_recv.at[j], dp_of(to_y, z, core), to_head)
        entry[4, j].start()

    def part_at(plane, e, of_core):
        first = (e % 2) * TOKENS + dp_of((y_hi + e // 2) % 2, plane, of_core) * BLOCK
        return kv_out.at[pl.ds(pl.multiple_of(first, 32), BLOCK), :]

    def plane_of(slot):
        return (z + PLANES - slot) % PLANES if slot <= 4 else (z + slot - 4) % PLANES

    ring, cross = {}, {}

    def to_twin(slot, e):
        part = part_at(plane_of(slot), e, core)
        cross[slot, e] = remote(part, part, c_send.at[slot, e], c_recv.at[slot, e], twin, head)
        cross[slot, e].start()

    def along(way, s, r):
        slot = s if way == 0 or s == 0 else 4 + s
        part = part_at(plane_of(slot), r, core)
        ring[way, s, r] = remote(
            part, part, r_send.at[way, s, r], r_recv.at[way, s, r], up if way == 0 else down, head)
        ring[way, s, r].start()

    def last_way(r):
        return 0 if r < 2 else 1

    top_out[...] = jnp.zeros_like(top_out)

    acc_out[...] = jnp.zeros_like(acc_out)
    tot_out[...] = jnp.zeros_like(tot_out)

    def look(slot, t, of_core):
        first = dp_of((y_hi + t) % 2, plane_of(slot), of_core) * BLOCK
        top_out[0, :, :] = jnp.maximum(top_out[0, :, :], squares_top(kv_out, first, BLOCK, slice(0, DH)))

    start_of = starts(lengths)
    second = second_first(start_of, z, core)

    def take(slot, of_core):
        plane = plane_of(slot)
        later = jnp.logical_and(second, z >= slot)

        def step(inner, carry):
            def chosen(first):
                low, high = (
                    kv_out[pl.ds(pl.multiple_of(first + dp_of(t, plane, of_core) * BLOCK, 32), BLOCK), :]
                    for t in range(2))
                return jnp.where(later, high, low)

            keys, values = chosen(0), chosen(TOKENS)
            key_first = (jnp.where(later, 16, 0) + dp_of(0, plane, of_core)) * BLOCK
            row_first = (jnp.where(second, 16, 0) + dp_of(0, z, core)) * BLOCK + inner * TQ
            rows = row_first + lax.broadcasted_iota(jnp.int32, (TQ, 1), 0)
            key_rows = key_first + lax.broadcasted_iota(jnp.int32, (1, BLOCK), 1)
            bias[...] = jnp.where((key_rows <= rows) & (key_rows >= start_of(rows)), 0.0, MASKED)
            for g in range(HALF):
                low, high = (
                    q_out[pl.ds(pl.multiple_of(t * BLOCK + inner * TQ, TQ), TQ), g * DH : (g + 1) * DH]
                    for t in range(2))
                scores = lax.dot_general(
                    jnp.where(second, high, low), keys, (((1,), (1,)), ((), ())),
                    preferred_element_type=jnp.float32) * SCALE
                weights = jnp.exp2(scores + bias[...])
                sums = weights[:, :DH]
                for w in range(1, BLOCK // DH):
                    sums = sums + weights[:, w * DH : (w + 1) * DH]
                part = pl.ds(g * TQ, TQ)
                tot_out[inner, part, :] += sums
                acc_out[inner, part, :] += jnp.dot(
                    weights.astype(jnp.bfloat16), values, preferred_element_type=jnp.float32)
            return carry

        lax.fori_loop(0, BLOCK // TQ, step, 0)

    for r in range(4):
        for j in range(8):
            if j or r >= 2:
                entry[r, j].wait_recv()
            else:
                entry[r, j].wait()
        along(0, 0, r)
        along(1, 0, r)
        to_twin(0, r)

    def close(slot):
        for e in range(4):
            cross[slot, e].wait_recv()
        for t in range(2):
            look(slot, t, core)
            look(slot, t, 1 - core)

    def arrive(s, r, way):
        slot = s if way == 0 or s == 4 else 4 + s
        ring[way, s - 1, r].wait_recv()
        if s < 3 or (s == 3 and way == last_way(r)):
            along(way, s, r)
        to_twin(slot, r)

    def both(s, r):
        for way in range(2):
            if s < 4 or way == last_way(r):
                arrive(s, r, way)

    close(0)
    for r in range(4):
        both(1, r)
    both(2, 0)
    close(1)
    both(2, 1)
    close(5)
    own_copy.wait()
    for j in range(1, 16):
        entry[4, j].wait_recv()
    for g in range(HALF):
        top_out[1, :, :] = jnp.maximum(
            top_out[1, :, :], squares_top(q_out, 0, 2 * BLOCK, slice(g * DH, (g + 1) * DH)))
    both(2, 2)
    take(0, core)
    both(2, 3)

    @pl.when(core == 1)
    def _():
        take(0, 0)

    both(3, 0)
    if NEAR >= 1:
        take(1, 0)
    both(3, 1)
    if NEAR >= 1:
        take(1, 1)
    both(3, 2)
    close(2)
    if NEAR >= 2:
        take(2, 0)
    both(3, 3)
    close(6)
    both(4, 0)
    both(4, 2)
    if NEAR >= 2:
        take(2, 1)
    both(4, 1)
    both(4, 3)
    close(3)
    if NEAR >= 3:
        take(3, 0)
        take(3, 1)
    close(7)
    close(4)
    for key, copy in entry.items():
        if key[0] < 2 and key[1] == 0:
            continue
        copy.wait_send()
    for group in (ring, cross):
        for copy in group.values():
            copy.wait_send()


def gather(lengths, q, k, v):
    q, k, v = (pltpu.with_memory_space_constraint(a, pltpu.HBM) for a in (q, k, v))
    return pl.pallas_call(
        gather_kernel,
        out_shape=(
            pltpu.VMEM((2 * BLOCK, WIDE), jnp.bfloat16),
            pltpu.VMEM((2 * TOKENS, DH), jnp.bfloat16),
            pltpu.VMEM((2, 8, DH), jnp.float32),
            pltpu.VMEM((BLOCK // TQ, HALF * TQ, DH), jnp.float32),
            pltpu.VMEM((BLOCK // TQ, HALF * TQ, DH), jnp.float32),
        ),
        in_specs=[pl.BlockSpec(memory_space=pltpu.SMEM)] + [pl.BlockSpec(memory_space=pltpu.HBM)] * 3,
        out_specs=[pl.BlockSpec(memory_space=pltpu.VMEM)] * 5,
        scratch_shapes=[
            pltpu.VMEM((2 * TOK, HK * DH), jnp.bfloat16),
            pltpu.VMEM((TQ, BLOCK), jnp.float32),
            pltpu.SemaphoreType.DMA((4, 8)),
            pltpu.SemaphoreType.DMA((4, 8)),
            pltpu.SemaphoreType.DMA((16,)),
            pltpu.SemaphoreType.DMA((16,)),
            pltpu.SemaphoreType.DMA((2, 4, 4)),
            pltpu.SemaphoreType.DMA((2, 4, 4)),
            pltpu.SemaphoreType.DMA((8, 4)),
            pltpu.SemaphoreType.DMA((8, 4)),
            pltpu.SemaphoreType.DMA((5,)),
        ],
        compiler_params=pltpu.CompilerParams(
            collective_id=0, has_side_effects=True, vmem_limit_bytes=12 * 1024 * 1024),
        name="gather",
    )(lengths, q, k, v)


def attend_kernel(lengths, q_ref, kv_ref, tops_ref, near_acc, near_tot, o_ref, acc, tot, top, bias):
    _, _, z, core, _ = place()
    start_of = starts(lengths)
    second = second_first(start_of, z, core)
    taken = jnp.maximum((2 * (z - NEAR) + jnp.where(second, 16, 0)) * BLOCK, 0)

    q_top, k_top = jnp.max(tops_ref[1, :, :]), jnp.max(tops_ref[0, :, :])
    small = q_top * k_top * 1.04 <= (BOUND * DH**0.5) ** 2

    def fold(row, first, width, masked, shifted):
        keys = kv_ref[pl.ds(pl.multiple_of(first, KS), width), :]
        values = kv_ref[pl.ds(pl.multiple_of(TOKENS + first, KS), width), :]
        if masked:
            positions = row[1] + lax.broadcasted_iota(jnp.int32, (TQ, 1), 0)
            key_positions = first + lax.broadcasted_iota(jnp.int32, (1, width), 1)
            allowed = (key_positions <= positions) & (key_positions >= start_of(positions))
            bias[:, :width] = jnp.where(allowed, 0.0, MASKED)
        for g in range(HALF):
            part = pl.ds(g * TQ, TQ)
            scores = lax.dot_general(
                q_ref[pl.ds(pl.multiple_of(row[0], TQ), TQ), g * DH : (g + 1) * DH], keys,
                (((1,), (1,)), ((), ())), preferred_element_type=jnp.float32) * SCALE
            if masked:
                scores = scores + bias[:, :width]
            if shifted:
                old = top[part, :]
                new = jnp.maximum(old, jnp.max(scores, axis=1, keepdims=True))
                top[part, :] = new
                weights = jnp.exp2(scores - new[:, :1])
                factor = jnp.exp2(old - new)
            else:
                weights = jnp.exp2(scores)
            if masked and shifted:
                weights = jnp.where(bias[:, :width] < 0.0, 0.0, weights)
            sums = weights[:, :DH]
            for n in range(1, width // DH):
                sums = sums + weights[:, n * DH : (n + 1) * DH]
            product = jnp.dot(weights.astype(jnp.bfloat16), values, preferred_element_type=jnp.float32)
            if shifted:
                tot[part, :] = tot[part, :] * factor + sums
                acc[part, :] = acc[part, :] * factor + product
            else:
                tot[part, :] += sums
                acc[part, :] += product

    def run(shifted):
        def tile(n, carry):
            block, inner = n // (BLOCK // TQ), n % (BLOCK // TQ)
            row = (n * TQ, dp_of(block, z, core) * BLOCK + inner * TQ)
            begin = row[1] // KS
            if shifted:
                acc[...] = jnp.zeros_like(acc)
                tot[...] = jnp.zeros_like(tot)
                top[...] = jnp.full_like(top, -1e30)
            else:
                near = (block == 1) == second

                @pl.when(near)
                def _():
                    acc[...] = near_acc[inner]
                    tot[...] = near_tot[inner]

                @pl.when(jnp.logical_not(near))
                def _():
                    acc[...] = jnp.zeros_like(acc)
                    tot[...] = jnp.zeros_like(tot)
                    fold(row, row[1], TQ, True, shifted)

                begin = jnp.where(near, jnp.minimum(begin, taken // KS), begin)
            low = start_of(row[1]) // KS
            high = jnp.minimum((start_of(row[1] + TQ - 1) + KS - 1) // KS, begin)
            wide = (begin - high) // (KT // KS)

            def at(width, masked, base):
                def body(i, c):
                    fold(row, (base + i * (width // KS)) * KS, width, masked, shifted)
                    return c
                return body

            if not shifted:
                cut = jnp.maximum(high - low, 0) // (KT // KS)
                lax.fori_loop(0, cut, at(KT, True, low), 0)
                low = low + cut * (KT // KS)
            lax.fori_loop(0, high - low, at(KS, True, low), 0)
            lax.fori_loop(0, wide, at(KT, False, high), 0)
            rest = high + wide * (KT // KS)
            lax.fori_loop(0, begin - rest, at(KS, False, rest), 0)
            if shifted:
                fold(row, row[1], TQ, True, shifted)
            for g in range(HALF):
                part = pl.ds(g * TQ, TQ)
                total = jnp.sum(tot[part, :], axis=1, keepdims=True)
                o_ref[pl.ds(pl.multiple_of(row[0], TQ), TQ), g * DH : (g + 1) * DH] = (
                    acc[part, :] / total).astype(jnp.bfloat16)
            return carry

        lax.fori_loop(0, 2 * BLOCK // TQ, tile, 0)

    @pl.when(small)
    def _():
        run(False)

    @pl.when(jnp.logical_not(small))
    def _():
        run(True)


def attend(lengths, *gathered):
    gathered = [pltpu.with_memory_space_constraint(a, pltpu.VMEM) for a in gathered]
    return pl.pallas_call(
        attend_kernel,
        out_shape=pltpu.VMEM((2 * BLOCK, WIDE), jnp.bfloat16),
        in_specs=[pl.BlockSpec(memory_space=pltpu.SMEM)] + [pl.BlockSpec(memory_space=pltpu.VMEM)] * 5,
        out_specs=pl.BlockSpec(memory_space=pltpu.VMEM),
        scratch_shapes=[pltpu.VMEM((HALF * TQ, DH), jnp.float32)] * 3 + [pltpu.VMEM((TQ, KT), jnp.float32)],
        compiler_params=pltpu.CompilerParams(vmem_limit_bytes=VMEM_LIMIT),
        name="attend",
    )(lengths, *gathered)


def scatter_kernel(o_ref, out_ref, send, recv, l_sem):
    dp, y_hi, z, core, head = place()
    peers = []
    for j in range(16):
        to_y = (y_hi + j // 8) % 2
        peers.append((dp_of(to_y, z, core), (head + j % 8) % 8, to_y))
    barrier = pltpu.get_barrier_semaphore()
    for to_dp, to_head, _ in peers[1:]:
        pl.semaphore_signal(barrier, inc=1, device_id=(to_dp, to_head), device_id_type=MESH)
    pl.semaphore_wait(barrier, 15)
    kv_head = head // 2 * 2 + y_hi
    columns = pl.ds(pl.multiple_of((kv_head * 2 + head % 2) * WIDE, 128), WIDE)
    copies = []
    for j in range(16):
        to_dp, to_head, to_y = peers[j]
        src = o_ref.at[pl.ds(pl.multiple_of(to_y * BLOCK + to_head * TOK, 32), TOK), :]
        if j == 0:
            copies.append(pltpu.make_async_copy(src, out_ref.at[:, columns], l_sem))
        else:
            copies.append(pltpu.make_async_remote_copy(
                src_ref=src, dst_ref=out_ref.at[:, columns], send_sem=send.at[j], recv_sem=recv.at[j],
                device_id=(to_dp, to_head), device_id_type=MESH))
        copies[-1].start()
    for copy in copies:
        copy.wait()


def scatter(o):
    return pl.pallas_call(
        scatter_kernel,
        out_shape=pltpu.VMEM((TOK, HQ * DH), jnp.bfloat16),
        in_specs=[pl.BlockSpec(memory_space=pltpu.VMEM)],
        out_specs=pl.BlockSpec(memory_space=pltpu.VMEM),
        scratch_shapes=[
            pltpu.SemaphoreType.DMA((16,)),
            pltpu.SemaphoreType.DMA((16,)),
            pltpu.SemaphoreType.DMA(()),
        ],
        compiler_params=pltpu.CompilerParams(collective_id=1, has_side_effects=True),
        name="scatter",
    )(pltpu.with_memory_space_constraint(o, pltpu.VMEM))


def on_device(queries, key_states, value_states, document_lengths):
    return scatter(attend(
        document_lengths, *gather(document_lengths, queries, key_states, value_states)))


def solution(mesh):
    placed = (P(("dp", "head"), None), P(("dp", "head"), None), P(("dp", "head"), None), P())
    return jax.shard_map(
        on_device, mesh=mesh, in_specs=placed, out_specs=P(("dp", "head"), None), check_vma=False
    )
```

```python
import jax
import jax.numpy as jnp
from jax import lax
from jax.experimental import pallas as pl
from jax.experimental.pallas import tpu as pltpu
from jax.sharding import PartitionSpec as P

HQ = 64
HK = 8
DH = 128
DOCS = 8
TOK = 96
BLOCK = 8 * TOK
TOKENS = 32 * BLOCK
PLANES = 8
GROUP = HQ // HK
HALF = GROUP // 2
WIDE = HALF * DH
TQ = 256
KT = 1024
KB = 2048
KS = 256
MASKED = -1e30
NEAR = 2
SCALE = DH**-0.5 * 1.4426950408889634
BOUND = 60.0
MESH = pl.DeviceIdType.MESH
VMEM_LIMIT = 16 * 1024 * 1024


def place():
    dp = lax.axis_index("dp")
    return dp, dp // 16, (dp % 16) // 2, dp % 2, lax.axis_index("head")


def dp_of(y_hi, z, core):
    return y_hi * 16 + z * 2 + core


def starts(lengths):
    ends = []
    running = jnp.int32(0)
    for d in range(DOCS):
        running = running + lengths[d]
        ends.append(running)
    return lambda position: sum(jnp.where(ends[d] <= position, lengths[d], 0) for d in range(DOCS))


def second_first(start_of, z, core):
    first, second = (dp_of(t, z, core) * BLOCK + BLOCK - 1 for t in range(2))
    return second - start_of(second) > first - start_of(first)


def squares_top(ref, first, rows, columns):
    ones = jnp.ones((DH, DH), jnp.bfloat16)

    def step(n, top):
        part = ref[pl.ds(pl.multiple_of(first + n * 384, 32), 384), columns].astype(jnp.float32)
        squares = jnp.dot((part * part).astype(jnp.bfloat16), ones, preferred_element_type=jnp.float32)
        return jnp.maximum(top, jnp.max(squares.reshape(48, 8, DH), axis=0))

    return lax.fori_loop(0, rows // 384, step, jnp.zeros((8, DH), jnp.float32))


def gather_kernel(
    lengths, q_ref, k_ref, v_ref, q_out, kv_out, top_out, acc_out, tot_out,
    kv_own, bias, a_send, a_recv, q_send, q_recv, r_send, r_recv, c_send, c_recv, l_sem
):
    dp, y_hi, z, core, head = place()

    def remote(src, dst, send, recv, to_dp, to_head):
        return pltpu.make_async_remote_copy(
            src_ref=src, dst_ref=dst, send_sem=send, recv_sem=recv,
            device_id=(to_dp, to_head), device_id_type=MESH,
        )

    def shifted(j):
        return (y_hi + j // 8) % 2, (head + j % 8) % 8

    up = dp_of(y_hi, (z + 1) % PLANES, core)
    down = dp_of(y_hi, (z + PLANES - 1) % PLANES, core)
    twin = dp_of(y_hi, z, 1 - core)

    def columns(first, width):
        return pl.ds(pl.multiple_of(first, 128), width)

    def q_place(to_y, to_head):
        src = q_ref.at[:, columns(((to_head // 2 * 2 + to_y) * 2 + to_head % 2) * WIDE, WIDE)]
        return src, q_out.at[pl.ds(pl.multiple_of(y_hi * BLOCK + head * TOK, 32), TOK), :]

    loads = [pltpu.make_async_copy(ref, kv_own.at[pl.ds(i * TOK, TOK), :], l_sem.at[i])
             for i, ref in enumerate((k_ref, v_ref))]
    for load in loads:
        load.start()
    barrier = pltpu.get_barrier_semaphore()
    for j in range(1, 16):
        to_y, to_head = shifted(j)
        pl.semaphore_signal(
            barrier, inc=1, device_id=(dp_of(to_y, z, core), to_head), device_id_type=MESH)
    for to_dp in (up, down, twin):
        pl.semaphore_signal(barrier, inc=1, device_id=(to_dp, head), device_id_type=MESH)
    own_q = q_place(y_hi, head)
    own_copy = pltpu.make_async_copy(own_q[0], own_q[1], l_sem.at[2])
    own_copy.start()
    for load in loads:
        load.wait()
    pl.semaphore_wait(barrier, 18)

    def class_ends(e, to_y, to_head):
        i = e % 2
        src = kv_own.at[pl.ds(pl.multiple_of(i * TOK, 32), TOK), columns((to_head // 2 * 2 + to_y) * DH, DH)]
        return src, kv_out.at[pl.ds(pl.multiple_of(i * TOKENS + dp * BLOCK + head * TOK, 32), TOK), :]

    entry = {}
    for e in range(4):
        to_y = (y_hi + e // 2) % 2
        for j in range(8):
            to_head = (head + j) % 8
            src, dst = class_ends(e, to_y, to_head)
            if j or e >= 2:
                entry[e, j] = remote(
                    src, dst, a_send.at[e, j], a_recv.at[e, j], dp_of(to_y, z, core), to_head)
            else:
                entry[e, j] = pltpu.make_async_copy(src, dst, l_sem.at[3 + e])
            entry[e, j].start()
    for j in range(1, 16):
        to_y, to_head = shifted(j)
        src, dst = q_place(to_y, to_head)
        entry[4, j] = remote(src, dst, q_send.at[j], q_recv.at[j], dp_of(to_y, z, core), to_head)
        entry[4, j].start()

    def part_at(plane, e, of_core):
        first = (e % 2) * TOKENS + dp_of((y_hi + e // 2) % 2, plane, of_core) * BLOCK
        return kv_out.at[pl.ds(pl.multiple_of(first, 32), BLOCK), :]

    def plane_of(slot):
        return (z + PLANES - slot) % PLANES if slot <= 4 else (z + slot - 4) % PLANES

    ring, cross = {}, {}

    def to_twin(slot, e):
        part = part_at(plane_of(slot), e, core)
        cross[slot, e] = remote(part, part, c_send.at[slot, e], c_recv.at[slot, e], twin, head)
        cross[slot, e].start()

    def along(way, s, r):
        slot = s if way == 0 or s == 0 else 4 + s
        part = part_at(plane_of(slot), r, core)
        ring[way, s, r] = remote(
            part, part, r_send.at[way, s, r], r_recv.at[way, s, r], up if way == 0 else down, head)
        ring[way, s, r].start()

    def last_way(r):
        return 0 if r < 2 else 1

    top_out[...] = jnp.zeros_like(top_out)

    acc_out[...] = jnp.zeros_like(acc_out)
    tot_out[...] = jnp.zeros_like(tot_out)

    def look(slot):
        ones = jnp.ones((DH, DH), jnp.bfloat16)
        tops = []
        for t in range(2):
            for of_core in range(2):
                first = dp_of(t, plane_of(slot), of_core) * BLOCK
                part = kv_out[pl.ds(pl.multiple_of(first, 32), BLOCK), :].astype(jnp.float32)
                squares = jnp.dot(
                    (part * part).astype(jnp.bfloat16), ones, preferred_element_type=jnp.float32)
                tops.append(jnp.max(squares.reshape(BLOCK // 8, 8, DH), axis=0))
        top = jnp.maximum(jnp.maximum(tops[0], tops[1]), jnp.maximum(tops[2], tops[3]))
        top_out[0, :, :] = jnp.maximum(top_out[0, :, :], top)

    start_of = starts(lengths)
    second = second_first(start_of, z, core)

    def take(slot, of_core):
        plane = plane_of(slot)
        later = jnp.logical_and(second, z >= slot)

        def step(inner, carry):
            def chosen(first):
                low, high = (
                    kv_out[pl.ds(pl.multiple_of(first + dp_of(t, plane, of_core) * BLOCK, 32), BLOCK), :]
                    for t in range(2))
                return jnp.where(later, high, low)

            keys, values = chosen(0), chosen(TOKENS)
            key_first = (jnp.where(later, 16, 0) + dp_of(0, plane, of_core)) * BLOCK
            row_first = (jnp.where(second, 16, 0) + dp_of(0, z, core)) * BLOCK + inner * TQ
            rows = row_first + lax.broadcasted_iota(jnp.int32, (TQ, 1), 0)
            key_rows = key_first + lax.broadcasted_iota(jnp.int32, (1, BLOCK), 1)
            bias[...] = jnp.where((key_rows <= rows) & (key_rows >= start_of(rows)), 0.0, MASKED)
            for g in range(HALF):
                low, high = (
                    q_out[pl.ds(pl.multiple_of(t * BLOCK + inner * TQ, TQ), TQ), g * DH : (g + 1) * DH]
                    for t in range(2))
                scores = lax.dot_general(
                    jnp.where(second, high, low), keys, (((1,), (1,)), ((), ())),
                    preferred_element_type=jnp.float32) * SCALE
                weights = jnp.exp2(scores + bias[...])
                sums = weights[:, :DH]
                for w in range(1, BLOCK // DH):
                    sums = sums + weights[:, w * DH : (w + 1) * DH]
                part = pl.ds(g * TQ, TQ)
                tot_out[inner, part, :] += sums
                acc_out[inner, part, :] += jnp.dot(
                    weights.astype(jnp.bfloat16), values, preferred_element_type=jnp.float32)
            return carry

        lax.fori_loop(0, BLOCK // TQ, step, 0)

    for r in range(4):
        for j in range(8):
            if j or r >= 2:
                entry[r, j].wait_recv()
            else:
                entry[r, j].wait()
        along(0, 0, r)
        along(1, 0, r)
        to_twin(0, r)

    def close(slot):
        for e in range(4):
            cross[slot, e].wait_recv()
        look(slot)

    def arrive(s, r, way):
        slot = s if way == 0 or s == 4 else 4 + s
        ring[way, s - 1, r].wait_recv()
        if s < 3 or (s == 3 and way == last_way(r)):
            along(way, s, r)
        to_twin(slot, r)

    def both(s, r):
        for way in range(2):
            if s < 4 or way == last_way(r):
                arrive(s, r, way)

    close(0)
    for r in range(4):
        both(1, r)
    both(2, 0)
    close(1)
    both(2, 1)
    close(5)
    own_copy.wait()
    for j in range(1, 16):
        entry[4, j].wait_recv()
    for g in range(HALF):
        top_out[1, :, :] = jnp.maximum(
            top_out[1, :, :], squares_top(q_out, 0, 2 * BLOCK, slice(g * DH, (g + 1) * DH)))
    both(2, 2)
    take(0, core)
    both(2, 3)

    @pl.when(core == 1)
    def _():
        take(0, 0)

    both(3, 0)
    if NEAR >= 1:
        take(1, 0)
    both(3, 1)
    if NEAR >= 1:
        take(1, 1)
    both(3, 2)
    close(2)
    if NEAR >= 2:
        take(2, 0)
    both(3, 3)
    close(6)
    both(4, 0)
    both(4, 2)
    if NEAR >= 2:
        take(2, 1)
    both(4, 1)
    both(4, 3)
    close(3)
    if NEAR >= 3:
        take(3, 0)
        take(3, 1)
    close(7)
    close(4)
    for key, copy in entry.items():
        if key[0] < 2 and key[1] == 0:
            continue
        copy.wait_send()
    for group in (ring, cross):
        for copy in group.values():
            copy.wait_send()


def gather(lengths, q, k, v):
    q, k, v = (pltpu.with_memory_space_constraint(a, pltpu.HBM) for a in (q, k, v))
    return pl.pallas_call(
        gather_kernel,
        out_shape=(
            pltpu.VMEM((2 * BLOCK, WIDE), jnp.bfloat16),
            pltpu.VMEM((2 * TOKENS, DH), jnp.bfloat16),
            pltpu.VMEM((2, 8, DH), jnp.float32),
            pltpu.VMEM((BLOCK // TQ, HALF * TQ, DH), jnp.float32),
            pltpu.VMEM((BLOCK // TQ, HALF * TQ, DH), jnp.float32),
        ),
        in_specs=[pl.BlockSpec(memory_space=pltpu.SMEM)] + [pl.BlockSpec(memory_space=pltpu.HBM)] * 3,
        out_specs=[pl.BlockSpec(memory_space=pltpu.VMEM)] * 5,
        scratch_shapes=[
            pltpu.VMEM((2 * TOK, HK * DH), jnp.bfloat16),
            pltpu.VMEM((TQ, BLOCK), jnp.float32),
            pltpu.SemaphoreType.DMA((4, 8)),
            pltpu.SemaphoreType.DMA((4, 8)),
            pltpu.SemaphoreType.DMA((16,)),
            pltpu.SemaphoreType.DMA((16,)),
            pltpu.SemaphoreType.DMA((2, 4, 4)),
            pltpu.SemaphoreType.DMA((2, 4, 4)),
            pltpu.SemaphoreType.DMA((8, 4)),
            pltpu.SemaphoreType.DMA((8, 4)),
            pltpu.SemaphoreType.DMA((5,)),
        ],
        compiler_params=pltpu.CompilerParams(
            collective_id=0, has_side_effects=True, vmem_limit_bytes=12 * 1024 * 1024),
        name="gather",
    )(lengths, q, k, v)


def attend_kernel(lengths, q_ref, kv_ref, tops_ref, near_acc, near_tot, o_ref, acc, tot, top, bias):
    _, _, z, core, _ = place()
    start_of = starts(lengths)
    second = second_first(start_of, z, core)
    taken = jnp.maximum((2 * (z - NEAR) + jnp.where(second, 16, 0)) * BLOCK, 0)

    q_top, k_top = jnp.max(tops_ref[1, :, :]), jnp.max(tops_ref[0, :, :])
    small = q_top * k_top * 1.04 <= (BOUND * DH**0.5) ** 2

    def fold(row, first, width, masked, shifted):
        keys = kv_ref[pl.ds(pl.multiple_of(first, KS), width), :]
        values = kv_ref[pl.ds(pl.multiple_of(TOKENS + first, KS), width), :]
        if masked:
            positions = row[1] + lax.broadcasted_iota(jnp.int32, (TQ, 1), 0)
            key_positions = first + lax.broadcasted_iota(jnp.int32, (1, width), 1)
            allowed = (key_positions <= positions) & (key_positions >= start_of(positions))
            bias[:, :width] = jnp.where(allowed, 0.0, MASKED)
        for g in range(HALF):
            part = pl.ds(g * TQ, TQ)
            scores = lax.dot_general(
                q_ref[pl.ds(pl.multiple_of(row[0], TQ), TQ), g * DH : (g + 1) * DH], keys,
                (((1,), (1,)), ((), ())), preferred_element_type=jnp.float32) * SCALE
            if masked:
                scores = scores + bias[:, :width]
            if shifted:
                old = top[part, :]
                new = jnp.maximum(old, jnp.max(scores, axis=1, keepdims=True))
                top[part, :] = new
                weights = jnp.exp2(scores - new[:, :1])
                factor = jnp.exp2(old - new)
            else:
                weights = jnp.exp2(scores)
            if masked and shifted:
                weights = jnp.where(bias[:, :width] < 0.0, 0.0, weights)
            sums = weights[:, :DH]
            for n in range(1, width // DH):
                sums = sums + weights[:, n * DH : (n + 1) * DH]
            product = jnp.dot(weights.astype(jnp.bfloat16), values, preferred_element_type=jnp.float32)
            if shifted:
                tot[part, :] = tot[part, :] * factor + sums
                acc[part, :] = acc[part, :] * factor + product
            else:
                tot[part, :] += sums
                acc[part, :] += product

    def run(shifted):
        def tile(n, carry):
            block, inner = n // (BLOCK // TQ), n % (BLOCK // TQ)
            row = (n * TQ, dp_of(block, z, core) * BLOCK + inner * TQ)
            begin = row[1] // KS
            if shifted:
                acc[...] = jnp.zeros_like(acc)
                tot[...] = jnp.zeros_like(tot)
                top[...] = jnp.full_like(top, -1e30)
            else:
                near = (block == 1) == second

                @pl.when(near)
                def _():
                    acc[...] = near_acc[inner]
                    tot[...] = near_tot[inner]

                @pl.when(jnp.logical_not(near))
                def _():
                    acc[...] = jnp.zeros_like(acc)
                    tot[...] = jnp.zeros_like(tot)
                    fold(row, row[1], TQ, True, shifted)

                begin = jnp.where(near, jnp.minimum(begin, taken // KS), begin)
            low = start_of(row[1]) // KS
            high = jnp.minimum((start_of(row[1] + TQ - 1) + KS - 1) // KS, begin)
            wide = (begin - high) // (KT // KS)

            def at(width, masked, base):
                def body(i, c):
                    fold(row, (base + i * (width // KS)) * KS, width, masked, shifted)
                    return c
                return body

            if not shifted:
                cut = jnp.maximum(high - low, 0) // (KT // KS)
                lax.fori_loop(0, cut, at(KT, True, low), 0)
                low = low + cut * (KT // KS)
            lax.fori_loop(0, high - low, at(KS, True, low), 0)
            if not shifted:
                broad = wide // (KB // KT)
                lax.fori_loop(0, broad, at(KB, False, high), 0)
                high, wide = high + broad * (KB // KS), wide - broad * (KB // KT)
            lax.fori_loop(0, wide, at(KT, False, high), 0)
            rest = high + wide * (KT // KS)
            lax.fori_loop(0, begin - rest, at(KS, False, rest), 0)
            if shifted:
                fold(row, row[1], TQ, True, shifted)
            for g in range(HALF):
                part = pl.ds(g * TQ, TQ)
                total = jnp.sum(tot[part, :], axis=1, keepdims=True)
                o_ref[pl.ds(pl.multiple_of(row[0], TQ), TQ), g * DH : (g + 1) * DH] = (
                    acc[part, :] / total).astype(jnp.bfloat16)
            return carry

        lax.fori_loop(0, 2 * BLOCK // TQ, tile, 0)

    @pl.when(small)
    def _():
        run(False)

    @pl.when(jnp.logical_not(small))
    def _():
        run(True)


def attend(lengths, *gathered):
    gathered = [pltpu.with_memory_space_constraint(a, pltpu.VMEM) for a in gathered]
    return pl.pallas_call(
        attend_kernel,
        out_shape=pltpu.VMEM((2 * BLOCK, WIDE), jnp.bfloat16),
        in_specs=[pl.BlockSpec(memory_space=pltpu.SMEM)] + [pl.BlockSpec(memory_space=pltpu.VMEM)] * 5,
        out_specs=pl.BlockSpec(memory_space=pltpu.VMEM),
        scratch_shapes=[pltpu.VMEM((HALF * TQ, DH), jnp.float32)] * 3 + [pltpu.VMEM((TQ, KT), jnp.float32)],
        compiler_params=pltpu.CompilerParams(vmem_limit_bytes=VMEM_LIMIT),
        name="attend",
    )(lengths, *gathered)


def scatter_kernel(o_ref, out_ref, send, recv, l_sem):
    dp, y_hi, z, core, head = place()
    peers = []
    for j in range(16):
        to_y = (y_hi + j // 8) % 2
        peers.append((dp_of(to_y, z, core), (head + j % 8) % 8, to_y))
    barrier = pltpu.get_barrier_semaphore()
    for to_dp, to_head, _ in peers[1:]:
        pl.semaphore_signal(barrier, inc=1, device_id=(to_dp, to_head), device_id_type=MESH)
    pl.semaphore_wait(barrier, 15)
    kv_head = head // 2 * 2 + y_hi
    columns = pl.ds(pl.multiple_of((kv_head * 2 + head % 2) * WIDE, 128), WIDE)
    copies = []
    for j in range(16):
        to_dp, to_head, to_y = peers[j]
        src = o_ref.at[pl.ds(pl.multiple_of(to_y * BLOCK + to_head * TOK, 32), TOK), :]
        if j == 0:
            copies.append(pltpu.make_async_copy(src, out_ref.at[:, columns], l_sem))
        else:
            copies.append(pltpu.make_async_remote_copy(
                src_ref=src, dst_ref=out_ref.at[:, columns], send_sem=send.at[j], recv_sem=recv.at[j],
                device_id=(to_dp, to_head), device_id_type=MESH))
        copies[-1].start()
    for copy in copies:
        copy.wait()


def scatter(o):
    return pl.pallas_call(
        scatter_kernel,
        out_shape=pltpu.VMEM((TOK, HQ * DH), jnp.bfloat16),
        in_specs=[pl.BlockSpec(memory_space=pltpu.VMEM)],
        out_specs=pl.BlockSpec(memory_space=pltpu.VMEM),
        scratch_shapes=[
            pltpu.SemaphoreType.DMA((16,)),
            pltpu.SemaphoreType.DMA((16,)),
            pltpu.SemaphoreType.DMA(()),
        ],
        compiler_params=pltpu.CompilerParams(collective_id=1, has_side_effects=True),
        name="scatter",
    )(pltpu.with_memory_space_constraint(o, pltpu.VMEM))


def on_device(queries, key_states, value_states, document_lengths):
    return scatter(attend(
        document_lengths, *gather(document_lengths, queries, key_states, value_states)))


def solution(mesh):
    placed = (P(("dp", "head"), None), P(("dp", "head"), None), P(("dp", "head"), None), P())
    return jax.shard_map(
        on_device, mesh=mesh, in_specs=placed, out_specs=P(("dp", "head"), None), check_vma=False
    )
```

```python
import jax
import jax.numpy as jnp
from jax import lax
from jax.experimental import pallas as pl
from jax.experimental.pallas import tpu as pltpu
from jax.sharding import PartitionSpec as P

HQ = 64
HK = 8
DH = 128
DOCS = 8
TOK = 96
BLOCK = 8 * TOK
TOKENS = 32 * BLOCK
PLANES = 8
GROUP = HQ // HK
HALF = GROUP // 2
WIDE = HALF * DH
TQ = 256
KT = 1024
KB = 2048
KS = 256
MASKED = -1e30
NEAR = 2
SCALE = DH**-0.5 * 1.4426950408889634
BOUND = 60.0
MESH = pl.DeviceIdType.MESH
FAR_FIRST = (12, 4, 11, 13, 10, 14, 3, 5, 8, 9, 15, 2, 6, 1, 7, 0)
VMEM_LIMIT = 16 * 1024 * 1024


def place():
    dp = lax.axis_index("dp")
    return dp, dp // 16, (dp % 16) // 2, dp % 2, lax.axis_index("head")


def dp_of(y_hi, z, core):
    return y_hi * 16 + z * 2 + core


def starts(lengths):
    ends = []
    running = jnp.int32(0)
    for d in range(DOCS):
        running = running + lengths[d]
        ends.append(running)
    return lambda position: sum(jnp.where(ends[d] <= position, lengths[d], 0) for d in range(DOCS))


def second_first(start_of, z, core):
    first, second = (dp_of(t, z, core) * BLOCK + BLOCK - 1 for t in range(2))
    return second - start_of(second) > first - start_of(first)


def squares_top(ref, first, rows, columns):
    ones = jnp.ones((DH, DH), jnp.bfloat16)

    def step(n, top):
        part = ref[pl.ds(pl.multiple_of(first + n * 384, 32), 384), columns].astype(jnp.float32)
        squares = jnp.dot((part * part).astype(jnp.bfloat16), ones, preferred_element_type=jnp.float32)
        return jnp.maximum(top, jnp.max(squares.reshape(48, 8, DH), axis=0))

    return lax.fori_loop(0, rows // 384, step, jnp.zeros((8, DH), jnp.float32))


def gather_kernel(
    lengths, q_ref, k_ref, v_ref, q_out, kv_out, top_out, acc_out, tot_out,
    kv_own, bias, a_send, a_recv, q_send, q_recv, r_send, r_recv, c_send, c_recv, l_sem
):
    dp, y_hi, z, core, head = place()

    def remote(src, dst, send, recv, to_dp, to_head):
        return pltpu.make_async_remote_copy(
            src_ref=src, dst_ref=dst, send_sem=send, recv_sem=recv,
            device_id=(to_dp, to_head), device_id_type=MESH,
        )

    def shifted(j):
        return (y_hi + j // 8) % 2, (head + j % 8) % 8

    up = dp_of(y_hi, (z + 1) % PLANES, core)
    down = dp_of(y_hi, (z + PLANES - 1) % PLANES, core)
    twin = dp_of(y_hi, z, 1 - core)

    def columns(first, width):
        return pl.ds(pl.multiple_of(first, 128), width)

    def q_place(to_y, to_head):
        src = q_ref.at[:, columns(((to_head // 2 * 2 + to_y) * 2 + to_head % 2) * WIDE, WIDE)]
        return src, q_out.at[pl.ds(pl.multiple_of(y_hi * BLOCK + head * TOK, 32), TOK), :]

    loads = [pltpu.make_async_copy(ref, kv_own.at[pl.ds(i * TOK, TOK), :], l_sem.at[i])
             for i, ref in enumerate((k_ref, v_ref))]
    for load in loads:
        load.start()
    barrier = pltpu.get_barrier_semaphore()
    for j in range(1, 16):
        to_y, to_head = shifted(j)
        pl.semaphore_signal(
            barrier, inc=1, device_id=(dp_of(to_y, z, core), to_head), device_id_type=MESH)
    for to_dp in (up, down, twin):
        pl.semaphore_signal(barrier, inc=1, device_id=(to_dp, head), device_id_type=MESH)
    own_q = q_place(y_hi, head)
    own_copy = pltpu.make_async_copy(own_q[0], own_q[1], l_sem.at[2])
    own_copy.start()
    for load in loads:
        load.wait()
    pl.semaphore_wait(barrier, 18)

    def class_ends(e, to_y, to_head):
        i = e % 2
        src = kv_own.at[pl.ds(pl.multiple_of(i * TOK, 32), TOK), columns((to_head // 2 * 2 + to_y) * DH, DH)]
        return src, kv_out.at[pl.ds(pl.multiple_of(i * TOKENS + dp * BLOCK + head * TOK, 32), TOK), :]

    entry = {}
    for e in range(4):
        to_y = (y_hi + e // 2) % 2
        for j in range(8):
            to_head = (head + j) % 8
            src, dst = class_ends(e, to_y, to_head)
            if j or e >= 2:
                entry[e, j] = remote(
                    src, dst, a_send.at[e, j], a_recv.at[e, j], dp_of(to_y, z, core), to_head)
            else:
                entry[e, j] = pltpu.make_async_copy(src, dst, l_sem.at[3 + e])
            entry[e, j].start()
    for j in range(1, 16):
        to_y, to_head = shifted(j)
        src, dst = q_place(to_y, to_head)
        entry[4, j] = remote(src, dst, q_send.at[j], q_recv.at[j], dp_of(to_y, z, core), to_head)
        entry[4, j].start()

    def part_at(plane, e, of_core):
        first = (e % 2) * TOKENS + dp_of((y_hi + e // 2) % 2, plane, of_core) * BLOCK
        return kv_out.at[pl.ds(pl.multiple_of(first, 32), BLOCK), :]

    def plane_of(slot):
        return (z + PLANES - slot) % PLANES if slot <= 4 else (z + slot - 4) % PLANES

    ring, cross = {}, {}

    def to_twin(slot, e):
        part = part_at(plane_of(slot), e, core)
        cross[slot, e] = remote(part, part, c_send.at[slot, e], c_recv.at[slot, e], twin, head)
        cross[slot, e].start()

    def along(way, s, r):
        slot = s if way == 0 or s == 0 else 4 + s
        part = part_at(plane_of(slot), r, core)
        ring[way, s, r] = remote(
            part, part, r_send.at[way, s, r], r_recv.at[way, s, r], up if way == 0 else down, head)
        ring[way, s, r].start()

    def last_way(r):
        return 0 if r < 2 else 1

    top_out[...] = jnp.zeros_like(top_out)

    acc_out[...] = jnp.zeros_like(acc_out)
    tot_out[...] = jnp.zeros_like(tot_out)

    def look(slot):
        ones = jnp.ones((DH, DH), jnp.bfloat16)
        tops = []
        for t in range(2):
            for of_core in range(2):
                first = dp_of(t, plane_of(slot), of_core) * BLOCK
                part = kv_out[pl.ds(pl.multiple_of(first, 32), BLOCK), :].astype(jnp.float32)
                squares = jnp.dot(
                    (part * part).astype(jnp.bfloat16), ones, preferred_element_type=jnp.float32)
                tops.append(jnp.max(squares.reshape(BLOCK // 8, 8, DH), axis=0))
        top = jnp.maximum(jnp.maximum(tops[0], tops[1]), jnp.maximum(tops[2], tops[3]))
        top_out[0, :, :] = jnp.maximum(top_out[0, :, :], top)

    start_of = starts(lengths)
    second = second_first(start_of, z, core)

    def take(slot, of_core):
        plane = plane_of(slot)
        later = jnp.logical_and(second, z >= slot)

        def step(inner, carry):
            def chosen(first):
                low, high = (
                    kv_out[pl.ds(pl.multiple_of(first + dp_of(t, plane, of_core) * BLOCK, 32), BLOCK), :]
                    for t in range(2))
                return jnp.where(later, high, low)

            keys, values = chosen(0), chosen(TOKENS)
            key_first = (jnp.where(later, 16, 0) + dp_of(0, plane, of_core)) * BLOCK
            row_first = (jnp.where(second, 16, 0) + dp_of(0, z, core)) * BLOCK + inner * TQ
            rows = row_first + lax.broadcasted_iota(jnp.int32, (TQ, 1), 0)
            key_rows = key_first + lax.broadcasted_iota(jnp.int32, (1, BLOCK), 1)
            bias[...] = jnp.where((key_rows <= rows) & (key_rows >= start_of(rows)), 0.0, MASKED)
            for g in range(HALF):
                low, high = (
                    q_out[pl.ds(pl.multiple_of(t * BLOCK + inner * TQ, TQ), TQ), g * DH : (g + 1) * DH]
                    for t in range(2))
                scores = lax.dot_general(
                    jnp.where(second, high, low), keys, (((1,), (1,)), ((), ())),
                    preferred_element_type=jnp.float32) * SCALE
                weights = jnp.exp2(scores + bias[...])
                sums = weights[:, :DH]
                for w in range(1, BLOCK // DH):
                    sums = sums + weights[:, w * DH : (w + 1) * DH]
                part = pl.ds(g * TQ, TQ)
                tot_out[inner, part, :] += sums
                acc_out[inner, part, :] += jnp.dot(
                    weights.astype(jnp.bfloat16), values, preferred_element_type=jnp.float32)
            return carry

        lax.fori_loop(0, BLOCK // TQ, step, 0)

    for r in range(4):
        for j in range(8):
            if j or r >= 2:
                entry[r, j].wait_recv()
            else:
                entry[r, j].wait()
        along(0, 0, r)
        along(1, 0, r)
        to_twin(0, r)

    def close(slot):
        for e in range(4):
            cross[slot, e].wait_recv()
        look(slot)

    def arrive(s, r, way):
        slot = s if way == 0 or s == 4 else 4 + s
        ring[way, s - 1, r].wait_recv()
        if s < 3 or (s == 3 and way == last_way(r)):
            along(way, s, r)
        to_twin(slot, r)

    def both(s, r):
        for way in range(2):
            if s < 4 or way == last_way(r):
                arrive(s, r, way)

    close(0)
    for r in range(4):
        both(1, r)
    both(2, 0)
    close(1)
    both(2, 1)
    close(5)
    own_copy.wait()
    for j in range(1, 16):
        entry[4, j].wait_recv()
    for g in range(HALF):
        top_out[1, :, :] = jnp.maximum(
            top_out[1, :, :], squares_top(q_out, 0, 2 * BLOCK, slice(g * DH, (g + 1) * DH)))
    both(2, 2)
    take(0, core)
    both(2, 3)

    @pl.when(core == 1)
    def _():
        take(0, 0)

    both(3, 0)
    if NEAR >= 1:
        take(1, 0)
    both(3, 1)
    if NEAR >= 1:
        take(1, 1)
    both(3, 2)
    close(2)
    if NEAR >= 2:
        take(2, 0)
    both(3, 3)
    close(6)
    both(4, 0)
    both(4, 2)
    if NEAR >= 2:
        take(2, 1)
    both(4, 1)
    both(4, 3)
    close(3)
    if NEAR >= 3:
        take(3, 0)
        take(3, 1)
    close(7)
    close(4)
    for key, copy in entry.items():
        if key[0] < 2 and key[1] == 0:
            continue
        copy.wait_send()
    for group in (ring, cross):
        for copy in group.values():
            copy.wait_send()


def gather(lengths, q, k, v):
    q, k, v = (pltpu.with_memory_space_constraint(a, pltpu.HBM) for a in (q, k, v))
    return pl.pallas_call(
        gather_kernel,
        out_shape=(
            pltpu.VMEM((2 * BLOCK, WIDE), jnp.bfloat16),
            pltpu.VMEM((2 * TOKENS, DH), jnp.bfloat16),
            pltpu.VMEM((2, 8, DH), jnp.float32),
            pltpu.VMEM((BLOCK // TQ, HALF * TQ, DH), jnp.float32),
            pltpu.VMEM((BLOCK // TQ, HALF * TQ, DH), jnp.float32),
        ),
        in_specs=[pl.BlockSpec(memory_space=pltpu.SMEM)] + [pl.BlockSpec(memory_space=pltpu.HBM)] * 3,
        out_specs=[pl.BlockSpec(memory_space=pltpu.VMEM)] * 5,
        scratch_shapes=[
            pltpu.VMEM((2 * TOK, HK * DH), jnp.bfloat16),
            pltpu.VMEM((TQ, BLOCK), jnp.float32),
            pltpu.SemaphoreType.DMA((4, 8)),
            pltpu.SemaphoreType.DMA((4, 8)),
            pltpu.SemaphoreType.DMA((16,)),
            pltpu.SemaphoreType.DMA((16,)),
            pltpu.SemaphoreType.DMA((2, 4, 4)),
            pltpu.SemaphoreType.DMA((2, 4, 4)),
            pltpu.SemaphoreType.DMA((8, 4)),
            pltpu.SemaphoreType.DMA((8, 4)),
            pltpu.SemaphoreType.DMA((5,)),
        ],
        compiler_params=pltpu.CompilerParams(
            collective_id=0, has_side_effects=True, vmem_limit_bytes=12 * 1024 * 1024),
        name="gather",
    )(lengths, q, k, v)


def attend_kernel(lengths, q_ref, kv_ref, tops_ref, near_acc, near_tot, o_ref, acc, tot, top, bias):
    _, _, z, core, _ = place()
    start_of = starts(lengths)
    second = second_first(start_of, z, core)
    taken = jnp.maximum((2 * (z - NEAR) + jnp.where(second, 16, 0)) * BLOCK, 0)

    q_top, k_top = jnp.max(tops_ref[1, :, :]), jnp.max(tops_ref[0, :, :])
    small = q_top * k_top * 1.04 <= (BOUND * DH**0.5) ** 2

    def fold(row, first, width, masked, shifted):
        keys = kv_ref[pl.ds(pl.multiple_of(first, KS), width), :]
        values = kv_ref[pl.ds(pl.multiple_of(TOKENS + first, KS), width), :]
        if masked:
            positions = row[1] + lax.broadcasted_iota(jnp.int32, (TQ, 1), 0)
            key_positions = first + lax.broadcasted_iota(jnp.int32, (1, width), 1)
            allowed = (key_positions <= positions) & (key_positions >= start_of(positions))
            bias[:, :width] = jnp.where(allowed, 0.0, MASKED)
        for g in range(HALF):
            part = pl.ds(g * TQ, TQ)
            scores = lax.dot_general(
                q_ref[pl.ds(pl.multiple_of(row[0], TQ), TQ), g * DH : (g + 1) * DH], keys,
                (((1,), (1,)), ((), ())), preferred_element_type=jnp.float32) * SCALE
            if masked:
                scores = scores + bias[:, :width]
            if shifted:
                old = top[part, :]
                new = jnp.maximum(old, jnp.max(scores, axis=1, keepdims=True))
                top[part, :] = new
                weights = jnp.exp2(scores - new[:, :1])
                factor = jnp.exp2(old - new)
            else:
                weights = jnp.exp2(scores)
            if masked and shifted:
                weights = jnp.where(bias[:, :width] < 0.0, 0.0, weights)
            sums = weights[:, :DH]
            for n in range(1, width // DH):
                sums = sums + weights[:, n * DH : (n + 1) * DH]
            product = jnp.dot(weights.astype(jnp.bfloat16), values, preferred_element_type=jnp.float32)
            if shifted:
                tot[part, :] = tot[part, :] * factor + sums
                acc[part, :] = acc[part, :] * factor + product
            else:
                tot[part, :] += sums
                acc[part, :] += product

    def run(shifted):
        def tile(n, carry):
            block, inner = n // (BLOCK // TQ), n % (BLOCK // TQ)
            row = (n * TQ, dp_of(block, z, core) * BLOCK + inner * TQ)
            begin = row[1] // KS
            if shifted:
                acc[...] = jnp.zeros_like(acc)
                tot[...] = jnp.zeros_like(tot)
                top[...] = jnp.full_like(top, -1e30)
            else:
                near = (block == 1) == second

                @pl.when(near)
                def _():
                    acc[...] = near_acc[inner]
                    tot[...] = near_tot[inner]

                @pl.when(jnp.logical_not(near))
                def _():
                    acc[...] = jnp.zeros_like(acc)
                    tot[...] = jnp.zeros_like(tot)
                    fold(row, row[1], TQ, True, shifted)

                begin = jnp.where(near, jnp.minimum(begin, taken // KS), begin)
            low = start_of(row[1]) // KS
            high = jnp.minimum((start_of(row[1] + TQ - 1) + KS - 1) // KS, begin)
            wide = (begin - high) // (KT // KS)

            def at(width, masked, base):
                def body(i, c):
                    fold(row, (base + i * (width // KS)) * KS, width, masked, shifted)
                    return c
                return body

            if not shifted:
                cut = jnp.maximum(high - low, 0) // (KT // KS)
                lax.fori_loop(0, cut, at(KT, True, low), 0)
                low = low + cut * (KT // KS)
            lax.fori_loop(0, high - low, at(KS, True, low), 0)
            if not shifted:
                broad = wide // (KB // KT)
                lax.fori_loop(0, broad, at(KB, False, high), 0)
                high, wide = high + broad * (KB // KS), wide - broad * (KB // KT)
            lax.fori_loop(0, wide, at(KT, False, high), 0)
            rest = high + wide * (KT // KS)
            lax.fori_loop(0, begin - rest, at(KS, False, rest), 0)
            if shifted:
                fold(row, row[1], TQ, True, shifted)
            for g in range(HALF):
                part = pl.ds(g * TQ, TQ)
                total = jnp.sum(tot[part, :], axis=1, keepdims=True)
                o_ref[pl.ds(pl.multiple_of(row[0], TQ), TQ), g * DH : (g + 1) * DH] = (
                    acc[part, :] / total).astype(jnp.bfloat16)
            return carry

        lax.fori_loop(0, 2 * BLOCK // TQ, tile, 0)

    @pl.when(small)
    def _():
        run(False)

    @pl.when(jnp.logical_not(small))
    def _():
        run(True)


def attend(lengths, *gathered):
    gathered = [pltpu.with_memory_space_constraint(a, pltpu.VMEM) for a in gathered]
    return pl.pallas_call(
        attend_kernel,
        out_shape=pltpu.VMEM((2 * BLOCK, WIDE), jnp.bfloat16),
        in_specs=[pl.BlockSpec(memory_space=pltpu.SMEM)] + [pl.BlockSpec(memory_space=pltpu.VMEM)] * 5,
        out_specs=pl.BlockSpec(memory_space=pltpu.VMEM),
        scratch_shapes=[pltpu.VMEM((HALF * TQ, DH), jnp.float32)] * 3 + [pltpu.VMEM((TQ, KT), jnp.float32)],
        compiler_params=pltpu.CompilerParams(vmem_limit_bytes=VMEM_LIMIT),
        name="attend",
    )(lengths, *gathered)


def scatter_kernel(o_ref, out_ref, send, recv, l_sem):
    dp, y_hi, z, core, head = place()
    peers = []
    for j in range(16):
        to_y = (y_hi + j // 8) % 2
        peers.append((dp_of(to_y, z, core), (head + j % 8) % 8, to_y))
    barrier = pltpu.get_barrier_semaphore()
    for to_dp, to_head, _ in peers[1:]:
        pl.semaphore_signal(barrier, inc=1, device_id=(to_dp, to_head), device_id_type=MESH)
    pl.semaphore_wait(barrier, 15)
    kv_head = head // 2 * 2 + y_hi
    columns = pl.ds(pl.multiple_of((kv_head * 2 + head % 2) * WIDE, 128), WIDE)
    copies = []
    for j in FAR_FIRST:
        to_dp, to_head, to_y = peers[j]
        src = o_ref.at[pl.ds(pl.multiple_of(to_y * BLOCK + to_head * TOK, 32), TOK), :]
        if j == 0:
            copies.append(pltpu.make_async_copy(src, out_ref.at[:, columns], l_sem))
        else:
            copies.append(pltpu.make_async_remote_copy(
                src_ref=src, dst_ref=out_ref.at[:, columns], send_sem=send.at[j], recv_sem=recv.at[j],
                device_id=(to_dp, to_head), device_id_type=MESH))
        copies[-1].start()
    for copy in copies:
        copy.wait()


def scatter(o):
    return pl.pallas_call(
        scatter_kernel,
        out_shape=pltpu.VMEM((TOK, HQ * DH), jnp.bfloat16),
        in_specs=[pl.BlockSpec(memory_space=pltpu.VMEM)],
        out_specs=pl.BlockSpec(memory_space=pltpu.VMEM),
        scratch_shapes=[
            pltpu.SemaphoreType.DMA((16,)),
            pltpu.SemaphoreType.DMA((16,)),
            pltpu.SemaphoreType.DMA(()),
        ],
        compiler_params=pltpu.CompilerParams(collective_id=1, has_side_effects=True),
        name="scatter",
    )(pltpu.with_memory_space_constraint(o, pltpu.VMEM))


def on_device(queries, key_states, value_states, document_lengths):
    return scatter(attend(
        document_lengths, *gather(document_lengths, queries, key_states, value_states)))


def solution(mesh):
    placed = (P(("dp", "head"), None), P(("dp", "head"), None), P(("dp", "head"), None), P())
    return jax.shard_map(
        on_device, mesh=mesh, in_specs=placed, out_specs=P(("dp", "head"), None), check_vma=False
    )
```
